32 devices in a mesh: dp: 16 (over z, y, core), tensor: 2 (over x).
Axes of the slice: x: 2, y: 2, z: 4, core: 2. Of those that a mesh axis runs over, the one named last changes fastest.
Arguments:
- normed_input: bfloat16 [2048, 8192], P('dp', 'tensor'), may hold values from -6 to 6
- key_cotangent: bfloat16 [2048, 1024], P('dp', 'tensor'), may hold values from -6 to 6
- frozen_key_weight: bfloat16 [8192, 1024], P(None, 'tensor'), may hold values from -0.1875 to 0.1875
- adapter_down_maps: bfloat16 [32, 8192, 16], P(None, 'tensor'), may hold values from -0.0625 to 0.0625
- adapter_up_maps: bfloat16 [32, 16, 1024], P(None, None, 'tensor'), may hold values from -0.1875 to 0.1875
- document_of_token: int32 [2048], P('dp'), may hold values from 0 to 31, never falling along the last dimension, each value on 1 to 512 neighbouring positions
- tenant_of_document: int32 [32], replicated, may hold values from 0 to 31
- tenant_slot_index: int32 [32], replicated, may hold values from 0 to 31, each once
Outputs:
- input_gradient: bfloat16 [2048, 8192], P('dp', 'tensor')
- down_gradient: bfloat16 [32, 8192, 16], P(None, 'tensor')
- up_gradient: bfloat16 [32, 16, 1024], P(None, None, 'tensor')
The draws below stay inside these ranges and needn't reach their ends.
Inputs may be any that keep to these rules, and one draw needn't show every extreme that they name: `document_of_token`: never falling along the tokens; each document 1 to (512) tokens. `tenant_slot_index`: each slot once.
All inputs are finite; a program needn't handle non-finite values.
Results may differ from the reference program's by a relative error of at most 0.008.
Values may be sent and summed in bfloat16 or wider, within the bound.
A program may use at most 64 MiB of HBM per device.

```python
import math
import jax
import jax.numpy as jnp
import numpy as np

MODEL_WIDTH = 8192
KEY_WIDTH = 1024
ADAPTER_RANK = 16
TENANT_COUNT = 32
TOK_DEV = 128
TOKENS = 2048
DOCS = 32


def touch_ends(values, own_key, low, high):
    spot = [jax.random.randint(jax.random.fold_in(own_key, axis), (), 0, length) for axis, length in enumerate(values.shape)]
    main_axis = values.shape.index(max(values.shape))
    next_to = spot[:main_axis] + [(spot[main_axis] + 1) % values.shape[main_axis]] + spot[main_axis + 1:]
    return values.at[tuple(spot)].set(low).at[tuple(next_to)].set(high)


def block_scale(key, dims, shards, low, high):
    def one(axis_at, shards_of):
        heights = jax.random.uniform(jax.random.fold_in(jax.random.fold_in(key, 6), axis_at), (shards_of,), jnp.float32, low / len(shards), high / len(shards))
        return jnp.repeat(jnp.exp(heights), dims[axis_at] // shards_of).reshape((-1,) + (1,) * (len(dims) - axis_at - 1))

    loudness = one(*shards[0])
    for cut in shards[1:]:
        loudness = loudness * one(*cut)
    return loudness


def rank_table(count, slope):
    weights = [(1 << 20) // math.isqrt(grade ** slope) + 1 for grade in range(1, count + 1)]
    scale = 1 + sum(weights) // (1 << 30)
    return np.cumsum(np.array([max(1, weight // scale) for weight in weights]))


def ranked(own_key, extent, number_of, lean):
    table = rank_table(number_of, lean)
    ticket = jax.random.randint(jax.random.fold_in(own_key, 1), extent, 0, int(table[number_of - 1]))
    grade = jnp.searchsorted(jnp.asarray(table, jnp.int32), ticket, side="right")
    return jax.random.permutation(jax.random.fold_in(own_key, 2), number_of)[grade].astype(jnp.int32)


def profile(number_of, total, most, slope):
    weights = [(1 << 20) // math.isqrt(rank ** slope) + 1 for rank in range(2, number_of + 1)]
    rest, given = total - most - (number_of - 1), [1] * (number_of - 1)
    while rest > 0:
        movable = [i for i in range(number_of - 1) if given[i] < most]
        whole, left = sum([weights[i] for i in movable]), rest
        for i in movable:
            extra = min(most - given[i], max(1, left * weights[i] // whole), rest)
            given[i] = given[i] + extra
            rest = rest - extra
    return np.array([most] + given)


def ragged_sizes(rng, number_of, total, bound, slope):
    if number_of == 2:
        one = jax.random.randint(rng, (), max(1, total - bound), min(bound, total - 1) + 1)
        return jnp.stack([one, total - one])
    sizes = jnp.asarray(profile(number_of, total, bound, slope), jnp.int32)
    twos = (number_of - 1) // 2
    giver, receiver = sizes[1:1 + 2 * twos:2], sizes[2:2 + 2 * twos:2]
    room = jnp.minimum(giver - 1, bound - receiver)
    shifted = jax.random.randint(jax.random.fold_in(rng, 1), (twos,), 0, 1 << 20) % (room + 1)
    sizes = sizes.at[1:1 + 2 * twos:2].set(giver - shifted).at[2:2 + 2 * twos:2].set(receiver + shifted)
    return sizes[jax.random.permutation(jax.random.fold_in(rng, 2), number_of)]


def gaussian(own_key, dims, deviation, most, split=(), held_as=jnp.bfloat16):
    level = block_scale(own_key, dims, split, -0.22, 0.18) if split else 1.0
    values = jax.random.normal(own_key, dims, jnp.float32) * deviation * level
    return jnp.minimum(jnp.maximum(values, -most), most).astype(held_as)


def setup_inputs(seed: int = 0) -> dict:
    seeds = jax.random.split(jax.random.key(seed), 9)
    return {
        "normed_input": gaussian(seeds[0], (TOKENS, MODEL_WIDTH), 1.0, 6.0, ((0, 16), (1, 2))),
        "key_cotangent": gaussian(seeds[1], (TOKENS, KEY_WIDTH), 1.0, 6.0, ((0, 16), (1, 2))),
        "frozen_key_weight": gaussian(seeds[2], (MODEL_WIDTH, KEY_WIDTH), KEY_WIDTH ** -0.5, 0.1875, ((1, 2),)),
        "adapter_down_maps": gaussian(seeds[3], (TENANT_COUNT, MODEL_WIDTH, ADAPTER_RANK), MODEL_WIDTH ** -0.5, 0.0625, ((1, 2),)),
        "adapter_up_maps": gaussian(seeds[4], (TENANT_COUNT, ADAPTER_RANK, KEY_WIDTH), KEY_WIDTH ** -0.5, 0.1875, ((2, 2),)),
        "document_of_token": jnp.searchsorted(jnp.cumsum(ragged_sizes(seeds[5], DOCS, TOKENS, 4 * TOK_DEV, 2)), jnp.arange(TOKENS), side="right").astype(jnp.int32),
        "tenant_of_document": touch_ends(ranked(seeds[6], (DOCS,), TENANT_COUNT, 2), jax.random.fold_in(seeds[6], 3), 0, TENANT_COUNT - 1).astype(jnp.int32),
        "tenant_slot_index": jax.random.permutation(seeds[7], TENANT_COUNT).astype(jnp.int32),
    }


adapter_scale = 2.0


def reference(normed_input, key_cotangent, frozen_key_weight, adapter_down_maps, adapter_up_maps, document_of_token, tenant_of_document, tenant_slot_index):
    tenant_count, model_width, adapter_rank = adapter_down_maps.shape
    slot = jnp.take(tenant_slot_index, jnp.take(tenant_of_document, document_of_token))
    member = (slot[:, None] == jnp.arange(tenant_count, dtype=jnp.int32)[None, :]).astype(jnp.float32)
    down_flattened = jnp.transpose(adapter_down_maps, (1, 0, 2)).reshape(model_width, tenant_count * adapter_rank)
    up_flattened = jnp.transpose(adapter_up_maps, (2, 0, 1)).reshape(adapter_up_maps.shape[2], tenant_count * adapter_rank)
    h_all = jnp.dot(normed_input, down_flattened, preferred_element_type=jnp.float32).reshape(-1, tenant_count, adapter_rank)
    g_all = jnp.dot(key_cotangent, up_flattened, preferred_element_type=jnp.float32).reshape(-1, tenant_count, adapter_rank)
    low_h = jnp.sum(h_all * member[:, :, None], axis=1).astype(jnp.bfloat16)
    low_g = jnp.sum(g_all * member[:, :, None], axis=1).astype(jnp.bfloat16)
    spread_hidden = (member[:, :, None] * low_h.astype(jnp.float32)[:, None, :]).astype(jnp.bfloat16).reshape(-1, tenant_count * adapter_rank)
    spread_cotangent = (member[:, :, None] * low_g.astype(jnp.float32)[:, None, :]).astype(jnp.bfloat16).reshape(-1, tenant_count * adapter_rank)
    frozen_output = jnp.dot(key_cotangent, frozen_key_weight.T, preferred_element_type=jnp.float32)
    adapter_output = jnp.dot(spread_cotangent, down_flattened.T, preferred_element_type=jnp.float32)
    input_gradient = (frozen_output + adapter_scale * adapter_output).astype(jnp.bfloat16)
    down_gradient = adapter_scale * jnp.dot(normed_input.T, spread_cotangent, preferred_element_type=jnp.float32)
    down_gradient = jnp.transpose(down_gradient.reshape(model_width, tenant_count, adapter_rank), (1, 0, 2)).astype(jnp.bfloat16)
    up_gradient = adapter_scale * jnp.dot(spread_hidden.T, key_cotangent, preferred_element_type=jnp.float32)
    up_gradient = up_gradient.reshape(tenant_count, adapter_rank, -1).astype(jnp.bfloat16)
    return input_gradient, down_gradient, up_gradient
```

```python
import jax
import jax.numpy as jnp
from jax import lax
from jax.sharding import PartitionSpec as P

adapter_scale = 2.0


def per_device(
    dp_count,
    tensor_count,
    normed_input,
    key_cotangent,
    frozen_key_weight,
    adapter_down_maps,
    adapter_up_maps,
    document_of_token,
    tenant_of_document,
    tenant_slot_index,
):
    tenant_count, token_rows, adapter_rank = adapter_down_maps.shape
    key_heads_width = adapter_up_maps.shape[2]
    tokens = normed_input.shape[0]
    doc_count = tenant_of_document.shape[0]
    pairs = tenant_count * adapter_rank
    bf16, f32 = jnp.bfloat16, jnp.float32
    tenants = jnp.arange(tenant_count, dtype=jnp.int32)
    slot_of_doc = jnp.sum(
        jnp.where(tenant_of_document[:, None] == tenants[None, :], tenant_slot_index[None, :], 0), axis=1
    )
    docs = jnp.arange(doc_count, dtype=jnp.int32)
    slot = jnp.sum(
        jnp.where(document_of_token[:, None] == docs[None, :], slot_of_doc[None, :], 0), axis=1
    )
    member = (slot[:, None] == tenants[None, :]).astype(f32)
    down_rows = jnp.transpose(adapter_down_maps, (0, 2, 1)).reshape(pairs, token_rows)
    up_rows = adapter_up_maps.reshape(pairs, key_heads_width)
    contract_last = (((1,), (1,)), ((), ()))
    h_all = lax.dot_general(normed_input, down_rows, contract_last, preferred_element_type=f32)
    g_all = lax.dot_general(key_cotangent, up_rows, contract_last, preferred_element_type=f32)
    h_part = jnp.sum(h_all.reshape(-1, tenant_count, adapter_rank) * member[:, :, None], axis=1)
    g_part = jnp.sum(g_all.reshape(-1, tenant_count, adapter_rank) * member[:, :, None], axis=1)
    low = lax.psum(jnp.concatenate([h_part, g_part], axis=1), "tensor").astype(bf16)

    x_all = lax.all_to_all(
        normed_input.reshape(tokens, dp_count, -1), "dp", split_axis=1, concat_axis=0, tiled=True
    ).reshape(tokens * dp_count, -1)
    k_all = lax.all_to_all(
        key_cotangent.reshape(tokens, dp_count, -1), "dp", split_axis=1, concat_axis=0, tiled=True
    ).reshape(tokens * dp_count, -1)
    tagged = jnp.concatenate([low, slot[:, None].astype(bf16)], axis=1)
    tagged_all = lax.all_gather(tagged, "dp", axis=0, tiled=True)
    slot_all = tagged_all[:, 2 * adapter_rank].astype(jnp.int32)
    member_all = (slot_all[:, None] == tenants[None, :]).astype(bf16)

    def spread(m, v):
        return (m[:, :, None] * v[:, None, :]).reshape(-1, pairs)

    spread_h = spread(member_all, tagged_all[:, :adapter_rank])
    spread_g_all = spread(member_all, tagged_all[:, adapter_rank : 2 * adapter_rank])
    contract_first = (((0,), (0,)), ((), ()))
    down_piece = (
        adapter_scale * lax.dot_general(spread_g_all, x_all, contract_first, preferred_element_type=f32)
    ).astype(bf16)
    up_piece = (
        adapter_scale * lax.dot_general(spread_h, k_all, contract_first, preferred_element_type=f32)
    ).astype(bf16)
    down_flat = lax.all_gather(down_piece, "dp", axis=1, tiled=True)
    up_flat = lax.all_gather(up_piece, "dp", axis=1, tiled=True)

    frozen = lax.dot_general(
        key_cotangent, frozen_key_weight, contract_last, preferred_element_type=f32
    )
    frozen_output = lax.psum_scatter(frozen.astype(bf16), "tensor", scatter_dimension=1, tiled=True)
    spread_g = spread(member.astype(bf16), low[:, adapter_rank:])
    adapter_output = jnp.dot(spread_g, down_rows, preferred_element_type=f32)
    input_gradient = (frozen_output.astype(f32) + adapter_scale * adapter_output).astype(bf16)
    down_gradient = jnp.transpose(
        down_flat.reshape(tenant_count, adapter_rank, token_rows), (0, 2, 1)
    )
    up_gradient = up_flat.reshape(tenant_count, adapter_rank, key_heads_width)
    return (input_gradient, down_gradient, up_gradient)


def solution(mesh):
    in_specs = (
        P("dp", "tensor"),
        P("dp", "tensor"),
        P(None, "tensor"),
        P(None, "tensor", None),
        P(None, None, "tensor"),
        P("dp"),
        P(),
        P(),
    )
    out_specs = (P("dp", "tensor"), P(None, "tensor", None), P(None, None, "tensor"))

    def body(*args):
        return per_device(mesh.shape["dp"], mesh.shape["tensor"], *args)

    return jax.shard_map(body, mesh=mesh, in_specs=in_specs, out_specs=out_specs, check_vma=False)
```

```python
import functools
import jax
import jax.numpy as jnp
from jax import lax
from jax.experimental import pallas as pl
from jax.experimental.pallas import tpu as pltpu
from jax.sharding import PartitionSpec as P

adapter_scale = 2.0


def per_device(
    dp_count,
    tensor_count,
    normed_input,
    key_cotangent,
    frozen_key_weight,
    adapter_down_maps,
    adapter_up_maps,
    document_of_token,
    tenant_of_document,
    tenant_slot_index,
):
    tenant_count, token_rows, adapter_rank = adapter_down_maps.shape
    key_heads_width = adapter_up_maps.shape[2]
    tokens = normed_input.shape[0]
    doc_count = tenant_of_document.shape[0]
    pairs = tenant_count * adapter_rank
    bf16, f32 = jnp.bfloat16, jnp.float32
    tenants = jnp.arange(tenant_count, dtype=jnp.int32)
    slot_of_doc = jnp.sum(
        jnp.where(tenant_of_document[:, None] == tenants[None, :], tenant_slot_index[None, :], 0), axis=1
    )
    docs = jnp.arange(doc_count, dtype=jnp.int32)
    slot = jnp.sum(
        jnp.where(document_of_token[:, None] == docs[None, :], slot_of_doc[None, :], 0), axis=1
    )
    member = (slot[:, None] == tenants[None, :]).astype(f32)
    down_rows = jnp.transpose(adapter_down_maps, (0, 2, 1)).reshape(pairs, token_rows)
    up_rows = adapter_up_maps.reshape(pairs, key_heads_width)
    contract_last = (((1,), (1,)), ((), ()))
    h_all = lax.dot_general(normed_input, down_rows, contract_last, preferred_element_type=f32)
    g_all = lax.dot_general(key_cotangent, up_rows, contract_last, preferred_element_type=f32)
    h_part = jnp.sum(h_all.reshape(-1, tenant_count, adapter_rank) * member[:, :, None], axis=1)
    g_part = jnp.sum(g_all.reshape(-1, tenant_count, adapter_rank) * member[:, :, None], axis=1)
    low = lax.psum(jnp.concatenate([h_part, g_part], axis=1), "tensor").astype(bf16)

    x_all = lax.all_to_all(
        normed_input.reshape(tokens, dp_count, -1), "dp", split_axis=1, concat_axis=0, tiled=True
    ).reshape(tokens * dp_count, -1)
    k_all = lax.all_to_all(
        key_cotangent.reshape(tokens, dp_count, -1), "dp", split_axis=1, concat_axis=0, tiled=True
    ).reshape(tokens * dp_count, -1)
    tagged = jnp.concatenate([low, slot[:, None].astype(bf16)], axis=1)
    tagged_all = lax.all_gather(tagged, "dp", axis=0, tiled=True)
    slot_all = tagged_all[:, 2 * adapter_rank].astype(jnp.int32)
    member_all = (slot_all[:, None] == tenants[None, :]).astype(bf16)

    def spread(m, v):
        return (m[:, :, None] * v[:, None, :]).reshape(-1, pairs)

    spread_h = spread(member_all, tagged_all[:, :adapter_rank])
    spread_g_all = spread(member_all, tagged_all[:, adapter_rank : 2 * adapter_rank])
    contract_first = (((0,), (0,)), ((), ()))
    down_piece = (
        adapter_scale * lax.dot_general(spread_g_all, x_all, contract_first, preferred_element_type=f32)
    ).astype(bf16)
    up_piece = (
        adapter_scale * lax.dot_general(spread_h, k_all, contract_first, preferred_element_type=f32)
    ).astype(bf16)
    down_flat = lax.all_gather(down_piece, "dp", axis=1, tiled=True)
    up_flat = lax.all_gather(up_piece, "dp", axis=1, tiled=True)

    frozen = lax.dot_general(
        key_cotangent, frozen_key_weight, contract_last, preferred_element_type=f32
    )
    frozen_output = lax.psum_scatter(frozen.astype(bf16), "tensor", scatter_dimension=1, tiled=True)
    spread_g = spread(member.astype(bf16), low[:, adapter_rank:])
    adapter_output = jnp.dot(spread_g, down_rows, preferred_element_type=f32)
    input_gradient = (frozen_output.astype(f32) + adapter_scale * adapter_output).astype(bf16)
    down_gradient = jnp.transpose(
        down_flat.reshape(tenant_count, adapter_rank, token_rows), (0, 2, 1)
    )
    up_gradient = up_flat.reshape(tenant_count, adapter_rank, key_heads_width)
    return (input_gradient, down_gradient, up_gradient)


MESH = pl.DeviceIdType.MESH


def kernel(
    dp,
    x_ref, kc_ref, kct_ref, up_ref, slot_ref, down_hbm, w_hbm,
    gathered_ref, ingrad_ref,
    down, w, x_all, kct_all, part, part_in, low_all, spread_h, spread_g, send_f, recv_f, own_f,
    local_sem, x_sem, k_sem, part_sem, low_sem, f_sem, z_sem, y_sem, c_sem,
):
    bf16, f32 = jnp.bfloat16, jnp.float32
    tokens, feats = x_ref.shape
    pairs = down.shape[0]
    heads = kc_ref.shape[1]
    rank = part.shape[0] // 2
    tenants = pairs // rank
    cols = feats // dp
    krows = heads // dp
    me = lax.axis_index("dp")
    ten = lax.axis_index("tensor")
    other = 1 - ten
    zn = dp // 4
    z, y, core = me // 4, (me // 2) % 2, me % 2

    def w_half(t, i):
        rows = pl.ds(pl.multiple_of(t * feats, feats), feats)
        return pltpu.make_async_copy(w_hbm.at[rows], w.at[i], local_sem.at[i])

    load_down = pltpu.make_async_copy(down_hbm, down, local_sem.at[2])
    load_down.start()
    load_other = w_half(other, 0)
    load_other.start()
    load_own = w_half(ten, 1)
    load_own.start()

    barrier = pltpu.get_barrier_semaphore()
    for o in range(1, dp):
        pl.semaphore_signal(
            barrier, inc=1, device_id=(lax.rem(me + o, dp), ten), device_id_type=MESH
        )
    pl.semaphore_signal(barrier, inc=1, device_id=(me, other), device_id_type=MESH)
    pl.semaphore_wait(barrier, dp)

    def remote(src, dst, sems, i, to):
        return pltpu.make_async_remote_copy(
            src_ref=src, dst_ref=dst, send_sem=sems.at[0, i], recv_sem=sems.at[1, i],
            device_id=to, device_id_type=MESH,
        )

    def span(i, n):
        return pl.ds(pl.multiple_of(i * n, n), n)

    x_copies, k_copies = [], []
    for o in range(1, dp):
        p = lax.rem(me + o, dp)
        c = remote(x_ref.at[:, span(p, cols)], x_all.at[span(me, tokens)], x_sem, o, (p, ten))
        c.start()
        x_copies.append(c)
        c = remote(
            kct_ref.at[span(p, krows)], kct_all.at[:, span(me, tokens)], k_sem, o, (p, ten)
        )
        c.start()
        k_copies.append(c)
    x_all[span(me, tokens), :] = x_ref[:, span(me, cols)]
    kct_all[:, span(me, tokens)] = kct_ref[span(me, krows), :]

    nt = (((1,), (1,)), ((), ()))
    slot_row = slot_ref[...].astype(f32)
    tenant_of_row = lax.broadcasted_iota(jnp.int32, (tenants, rank, tokens), 0).astype(f32)

    def pick(values):
        v = values.reshape(tenants, rank, tokens)
        return jnp.sum(jnp.where(tenant_of_row == slot_row[None], v, 0.0), axis=0)

    def spread(values, slots):
        full = jnp.where(tenant_of_row == slots[None], values[None], 0.0)
        return full.astype(bf16).reshape(pairs, tokens)

    part[rank:, :] = pick(lax.dot_general(up_ref[...], kc_ref[...], nt, preferred_element_type=f32))
    load_down.wait()
    part[:rank, :] = pick(lax.dot_general(down[...], x_ref[...], nt, preferred_element_type=f32))
    part_copy = remote(part, part_in, part_sem, 0, (me, other))
    part_copy.start()

    chunk = 512
    groups = f_sem.shape[1]
    per_group = feats // chunk // groups
    load_other.wait()
    f_copies = []
    for g in range(groups):

        @pl.loop(g * per_group, (g + 1) * per_group)
        def _(j):
            at = span(j, chunk)
            send_f[:, at] = lax.dot_general(
                kc_ref[...], w[0, at, :], nt, preferred_element_type=f32
            ).astype(bf16)

        width = per_group * chunk
        at = pl.ds(g * width, width)
        c = remote(send_f.at[:, at], recv_f.at[:, at], f_sem, g, (me, other))
        c.start()
        f_copies.append(c)

    part_copy.wait()
    total = part[...] + part_in[...]
    low_all[me, : 2 * rank, :] = total.astype(bf16)
    low_all[me, 2 * rank :, :] = jnp.broadcast_to(slot_row, (rank, tokens)).astype(bf16)
    low_copies = []
    for o in range(1, dp):
        c = remote(low_all.at[me], low_all.at[me], low_sem, o, (lax.rem(me + o, dp), ten))
        c.start()
        low_copies.append(c)

    low_g = total[rank:, :].astype(bf16).astype(f32)
    mine = spread(low_g, jnp.broadcast_to(slot_row, (rank, tokens)))
    tn = (((0,), (0,)), ((), ()))
    load_own.wait()

    @pl.loop(0, feats // chunk)
    def _(j):
        at = span(j, chunk)
        own_f[:, at] = lax.dot_general(
            kc_ref[...], w[1, at, :], nt, preferred_element_type=f32
        ) + adapter_scale * lax.dot_general(mine, down[:, at], tn, preferred_element_type=f32)

    for c in low_copies:
        c.wait()

    @pl.loop(0, dp)
    def _(s):
        at = span(s, tokens)
        slots = low_all[s, 2 * rank :, :].astype(f32)
        spread_h[:, at] = spread(low_all[s, :rank, :].astype(f32), slots)
        spread_g[:, at] = spread(low_all[s, rank : 2 * rank, :].astype(f32), slots)

    for c in k_copies:
        c.wait()
    up_piece = adapter_scale * lax.dot_general(
        kct_all[...], spread_h[...], nt, preferred_element_type=f32
    )
    folds = pairs // cols
    for i in range(folds):
        gathered_ref[pairs + i * krows : pairs + (i + 1) * krows, span(me, cols)] = up_piece[
            :, i * cols : (i + 1) * cols
        ].astype(bf16)
    for c in x_copies:
        c.wait()
    gathered_ref[:pairs, span(me, cols)] = (
        adapter_scale * jnp.dot(spread_g[...], x_all[...], preferred_element_type=f32)
    ).astype(bf16)

    half = gathered_ref.shape[0] // 2
    pending = []

    def block(src, h):
        return gathered_ref.at[pl.ds(h * half, half), span(src, cols)]

    def index(zz, yy, cc):
        return (zz * 2 + yy) * 2 + cc

    def push(src, h, sems, i, to):
        c = remote(block(src, h), block(src, h), sems, i, (to, ten))
        c.start()
        pending.append(c)
        return c

    right = index(lax.rem(z + 1, zn), y, core)
    left = index(lax.rem(z + zn - 1, zn), y, core)
    across = index(z, 1 - y, core)
    twin = index(z, y, 1 - core)

    def ring(step, h):
        away = zn - step if h == 0 else step
        src = index(lax.rem(z + away, zn), y, core)
        c = None
        if step < zn - 1:
            c = push(src, h, z_sem, 2 * step + h, right if h == 0 else left)
        i = 2 * step + h
        yc = push(src, h, y_sem, i, across)
        push(src, h, c_sem, i, twin)
        return c, yc, away

    now = [ring(0, h) for h in range(2)]

    for c in f_copies:
        c.wait()

    @pl.loop(0, feats // chunk)
    def _(j):
        at = span(j, chunk)
        ingrad_ref[:, at] = (own_f[:, at] + recv_f[:, at].astype(f32)).astype(bf16)

    for step in range(1, zn + 1):
        later = []
        for h in range(2):
            if step < zn:
                now[h][0].wait_recv()
                later.append(ring(step, h))
        for h in range(2):
            _, yc, away = now[h]
            yc.wait_recv()
            src = index(lax.rem(z + away, zn), 1 - y, core)
            push(src, h, c_sem, 2 * zn + 2 * (step - 1) + h, twin)
        now = later
    for c in pending:
        c.wait_send()
    for i in range(4 * zn):
        remote(block(0, 0), block(0, 0), c_sem, i, (twin, ten)).wait_recv()


def per_device_kernel(
    dp,
    normed_input,
    key_cotangent,
    frozen_key_weight,
    adapter_down_maps,
    adapter_up_maps,
    document_of_token,
    tenant_of_document,
    tenant_slot_index,
):
    tenant_count, feats, rank = adapter_down_maps.shape
    heads = adapter_up_maps.shape[2]
    tokens = normed_input.shape[0]
    pairs = tenant_count * rank
    cols = feats // dp
    krows = heads // dp
    zn = dp // 4
    rows = pairs + krows * (pairs // cols)
    bf16, f32 = jnp.bfloat16, jnp.float32
    tenants = jnp.arange(tenant_count, dtype=jnp.int32)
    slot_of_doc = jnp.sum(
        jnp.where(tenant_of_document[:, None] == tenants[None, :], tenant_slot_index[None, :], 0), axis=1
    )
    docs = jnp.arange(tenant_of_document.shape[0], dtype=jnp.int32)
    slot = jnp.sum(
        jnp.where(document_of_token[None, :] == docs[:, None], slot_of_doc[:, None], 0),
        axis=0,
        keepdims=True,
    )
    down_rows = jnp.transpose(adapter_down_maps, (0, 2, 1)).reshape(pairs, feats)
    up_rows = adapter_up_maps.reshape(pairs, heads)
    vmem = pl.BlockSpec(memory_space=pltpu.VMEM)
    hbm = pl.BlockSpec(memory_space=pl.ANY)
    dma = pltpu.SemaphoreType.DMA
    gathered, input_gradient = pl.pallas_call(
        functools.partial(kernel, dp),
        out_shape=(
            jax.ShapeDtypeStruct((rows, feats), bf16),
            jax.ShapeDtypeStruct((tokens, feats), bf16),
        ),
        in_specs=[vmem] * 5 + [hbm] * 2,
        out_specs=(vmem, vmem),
        scratch_shapes=[
            pltpu.VMEM((pairs, feats), bf16),
            pltpu.VMEM((2, feats, heads), bf16),
            pltpu.VMEM((tokens * dp, cols), bf16),
            pltpu.VMEM((krows, tokens * dp), bf16),
            pltpu.VMEM((2 * rank, tokens), f32),
            pltpu.VMEM((2 * rank, tokens), f32),
            pltpu.VMEM((dp, 3 * rank, tokens), bf16),
            pltpu.VMEM((pairs, tokens * dp), bf16),
            pltpu.VMEM((pairs, tokens * dp), bf16),
            pltpu.VMEM((tokens, feats), bf16),
            pltpu.VMEM((tokens, feats), bf16),
            pltpu.VMEM((tokens, feats), f32),
            dma((3,)),
            dma((2, dp)),
            dma((2, dp)),
            dma((2, 1)),
            dma((2, dp)),
            dma((2, 4)),
            dma((2, 2 * zn)),
            dma((2, 2 * zn)),
            dma((2, 4 * zn)),
        ],
        compiler_params=pltpu.CompilerParams(
            collective_id=0, has_side_effects=True, vmem_limit_bytes=60 * 1024 * 1024
        ),
    )(
        normed_input,
        key_cotangent,
        key_cotangent.T,
        up_rows,
        slot,
        down_rows,
        frozen_key_weight,
    )
    down_gradient = jnp.transpose(
        gathered[:pairs].reshape(tenant_count, rank, feats), (0, 2, 1)
    )
    up = gathered[pairs:].reshape(pairs // cols, krows, dp, cols)
    up_gradient = jnp.transpose(up, (0, 3, 2, 1)).reshape(tenant_count, rank, heads)
    return (input_gradient, down_gradient, up_gradient)


def fits_kernel(dp, tensor, args):
    tokens, feats = args[0].shape
    heads = args[1].shape[1]
    tenant_count, _, rank = args[3].shape
    pairs = tenant_count * rank
    if tensor != 2 or dp % 4 or dp < 8 or tokens != 128 or feats % (dp * 128) or heads % (dp * 16):
        return False
    cols = feats // dp
    rows = pairs + (heads // dp) * (pairs // cols)
    return (
        feats % 2048 == 0 and pairs % cols == 0 and rank % 16 == 0
        and rows % 32 == 0 and tenant_count <= 256
    )


def solution(mesh):
    in_specs = (
        P("dp", "tensor"),
        P("dp", "tensor"),
        P(None, "tensor"),
        P(None, "tensor", None),
        P(None, None, "tensor"),
        P("dp"),
        P(),
        P(),
    )
    out_specs = (P("dp", "tensor"), P(None, "tensor", None), P(None, None, "tensor"))

    def body(*args):
        dp, tensor = mesh.shape["dp"], mesh.shape["tensor"]
        if fits_kernel(dp, tensor, args):
            return per_device_kernel(dp, *args)
        return per_device(dp, tensor, *args)

    return jax.shard_map(body, mesh=mesh, in_specs=in_specs, out_specs=out_specs, check_vma=False)
```

```python
import functools
import jax
import jax.numpy as jnp
from jax import lax
from jax.experimental import pallas as pl
from jax.experimental.pallas import tpu as pltpu
from jax.sharding import PartitionSpec as P

adapter_scale = 2.0


def per_device(
    dp_count,
    tensor_count,
    normed_input,
    key_cotangent,
    frozen_key_weight,
    adapter_down_maps,
    adapter_up_maps,
    document_of_token,
    tenant_of_document,
    tenant_slot_index,
):
    tenant_count, token_rows, adapter_rank = adapter_down_maps.shape
    key_heads_width = adapter_up_maps.shape[2]
    tokens = normed_input.shape[0]
    doc_count = tenant_of_document.shape[0]
    pairs = tenant_count * adapter_rank
    bf16, f32 = jnp.bfloat16, jnp.float32
    tenants = jnp.arange(tenant_count, dtype=jnp.int32)
    slot_of_doc = jnp.sum(
        jnp.where(tenant_of_document[:, None] == tenants[None, :], tenant_slot_index[None, :], 0), axis=1
    )
    docs = jnp.arange(doc_count, dtype=jnp.int32)
    slot = jnp.sum(
        jnp.where(document_of_token[:, None] == docs[None, :], slot_of_doc[None, :], 0), axis=1
    )
    member = (slot[:, None] == tenants[None, :]).astype(f32)
    down_rows = jnp.transpose(adapter_down_maps, (0, 2, 1)).reshape(pairs, token_rows)
    up_rows = adapter_up_maps.reshape(pairs, key_heads_width)
    contract_last = (((1,), (1,)), ((), ()))
    h_all = lax.dot_general(normed_input, down_rows, contract_last, preferred_element_type=f32)
    g_all = lax.dot_general(key_cotangent, up_rows, contract_last, preferred_element_type=f32)
    h_part = jnp.sum(h_all.reshape(-1, tenant_count, adapter_rank) * member[:, :, None], axis=1)
    g_part = jnp.sum(g_all.reshape(-1, tenant_count, adapter_rank) * member[:, :, None], axis=1)
    low = lax.psum(jnp.concatenate([h_part, g_part], axis=1), "tensor").astype(bf16)

    x_all = lax.all_to_all(
        normed_input.reshape(tokens, dp_count, -1), "dp", split_axis=1, concat_axis=0, tiled=True
    ).reshape(tokens * dp_count, -1)
    k_all = lax.all_to_all(
        key_cotangent.reshape(tokens, dp_count, -1), "dp", split_axis=1, concat_axis=0, tiled=True
    ).reshape(tokens * dp_count, -1)
    tagged = jnp.concatenate([low, slot[:, None].astype(bf16)], axis=1)
    tagged_all = lax.all_gather(tagged, "dp", axis=0, tiled=True)
    slot_all = tagged_all[:, 2 * adapter_rank].astype(jnp.int32)
    member_all = (slot_all[:, None] == tenants[None, :]).astype(bf16)

    def spread(m, v):
        return (m[:, :, None] * v[:, None, :]).reshape(-1, pairs)

    spread_h = spread(member_all, tagged_all[:, :adapter_rank])
    spread_g_all = spread(member_all, tagged_all[:, adapter_rank : 2 * adapter_rank])
    contract_first = (((0,), (0,)), ((), ()))
    down_piece = (
        adapter_scale * lax.dot_general(spread_g_all, x_all, contract_first, preferred_element_type=f32)
    ).astype(bf16)
    up_piece = (
        adapter_scale * lax.dot_general(spread_h, k_all, contract_first, preferred_element_type=f32)
    ).astype(bf16)
    down_flat = lax.all_gather(down_piece, "dp", axis=1, tiled=True)
    up_flat = lax.all_gather(up_piece, "dp", axis=1, tiled=True)

    frozen = lax.dot_general(
        key_cotangent, frozen_key_weight, contract_last, preferred_element_type=f32
    )
    frozen_output = lax.psum_scatter(frozen.astype(bf16), "tensor", scatter_dimension=1, tiled=True)
    spread_g = spread(member.astype(bf16), low[:, adapter_rank:])
    adapter_output = jnp.dot(spread_g, down_rows, preferred_element_type=f32)
    input_gradient = (frozen_output.astype(f32) + adapter_scale * adapter_output).astype(bf16)
    down_gradient = jnp.transpose(
        down_flat.reshape(tenant_count, adapter_rank, token_rows), (0, 2, 1)
    )
    up_gradient = up_flat.reshape(tenant_count, adapter_rank, key_heads_width)
    return (input_gradient, down_gradient, up_gradient)


MESH = pl.DeviceIdType.MESH


def kernel(
    dp,
    x_ref, kc_ref, kct_ref, up_ref, slot_ref, down_hbm, w_hbm,
    down_out, up_out, ingrad_ref,
    gathered_ref, down, w, x_all, kct_all, part, part_in, low_all, spread_h, spread_g, send_f, recv_f, own_f,
    local_sem, x_sem, k_sem, part_sem, low_sem, f_sem, z_sem, y_sem, c_sem, out_sem,
):
    bf16, f32 = jnp.bfloat16, jnp.float32
    tokens, feats = x_ref.shape
    pairs = down.shape[0]
    heads = kc_ref.shape[1]
    rank = part.shape[0] // 2
    tenants = pairs // rank
    cols = feats // dp
    krows = heads // dp
    me = lax.axis_index("dp")
    ten = lax.axis_index("tensor")
    other = 1 - ten
    zn = dp // 4
    z, y, core = me // 4, (me // 2) % 2, me % 2

    def w_half(t, i):
        rows = pl.ds(pl.multiple_of(t * feats, feats), feats)
        return pltpu.make_async_copy(w_hbm.at[rows], w.at[i], local_sem.at[i])

    load_down = pltpu.make_async_copy(down_hbm, down, local_sem.at[2])
    load_down.start()
    load_other = w_half(other, 0)
    load_other.start()
    load_own = w_half(ten, 1)
    load_own.start()

    barrier = pltpu.get_barrier_semaphore()
    for o in range(1, dp):
        pl.semaphore_signal(
            barrier, inc=1, device_id=(lax.rem(me + o, dp), ten), device_id_type=MESH
        )
    pl.semaphore_signal(barrier, inc=1, device_id=(me, other), device_id_type=MESH)
    pl.semaphore_wait(barrier, dp)

    def remote(src, dst, sems, i, to):
        return pltpu.make_async_remote_copy(
            src_ref=src, dst_ref=dst, send_sem=sems.at[0, i], recv_sem=sems.at[1, i],
            device_id=to, device_id_type=MESH,
        )

    def span(i, n):
        return pl.ds(pl.multiple_of(i * n, n), n)

    half = cols // 2

    def half_of(src, h):
        return pl.ds(pl.multiple_of(src * cols + h * half, half), half)

    x_copies, k_copies = [[], []], []
    for o in range(1, dp):
        p = lax.rem(me + o, dp)
        c = remote(
            kct_ref.at[span(p, krows)], kct_all.at[:, span(me, tokens)], k_sem, o, (p, ten)
        )
        c.start()
        k_copies.append(c)
    for h in range(2):
        for o in range(1, dp):
            p = lax.rem(me + o, dp)
            c = remote(
                x_ref.at[:, half_of(p, h)],
                x_all.at[span(me, tokens), pl.ds(h * half, half)],
                x_sem,
                h * dp + o,
                (p, ten),
            )
            c.start()
            x_copies[h].append(c)
    x_all[span(me, tokens), :] = x_ref[:, span(me, cols)]
    kct_all[:, span(me, tokens)] = kct_ref[span(me, krows), :]

    nt = (((1,), (1,)), ((), ()))
    slot_row = slot_ref[...].astype(f32)
    tenant_of_row = lax.broadcasted_iota(jnp.int32, (tenants, rank, tokens), 0).astype(f32)

    def pick(values):
        v = values.reshape(tenants, rank, tokens)
        return jnp.sum(jnp.where(tenant_of_row == slot_row[None], v, 0.0), axis=0)

    def spread(values, slots):
        full = jnp.where(tenant_of_row == slots[None], values[None], 0.0)
        return full.astype(bf16).reshape(pairs, tokens)

    part[rank:, :] = pick(lax.dot_general(up_ref[...], kc_ref[...], nt, preferred_element_type=f32))
    load_down.wait()
    part[:rank, :] = pick(lax.dot_general(down[...], x_ref[...], nt, preferred_element_type=f32))
    part_copy = remote(part, part_in, part_sem, 0, (me, other))
    part_copy.start()

    chunk = 512
    groups = f_sem.shape[1]
    per_group = feats // chunk // groups
    load_other.wait()
    f_copies = []
    for g in range(groups):

        @pl.loop(g * per_group, (g + 1) * per_group)
        def _(j):
            at = span(j, chunk)
            send_f[:, at] = lax.dot_general(
                kc_ref[...], w[0, at, :], nt, preferred_element_type=f32
            ).astype(bf16)

        width = per_group * chunk
        at = pl.ds(g * width, width)
        c = remote(send_f.at[:, at], recv_f.at[:, at], f_sem, g, (me, other))
        c.start()
        f_copies.append(c)

    part_copy.wait()
    total = part[...] + part_in[...]
    low_all[me, : 2 * rank, :] = total.astype(bf16)
    low_all[me, 2 * rank :, :] = jnp.broadcast_to(slot_row, (rank, tokens)).astype(bf16)
    low_copies = []
    for o in range(1, dp):
        c = remote(low_all.at[me], low_all.at[me], low_sem, o, (lax.rem(me + o, dp), ten))
        c.start()
        low_copies.append(c)

    low_g = total[rank:, :].astype(bf16).astype(f32)
    mine = spread(low_g, jnp.broadcast_to(slot_row, (rank, tokens)))
    tn = (((0,), (0,)), ((), ()))
    load_own.wait()

    @pl.loop(0, feats // chunk)
    def _(j):
        at = span(j, chunk)
        own_f[:, at] = lax.dot_general(
            kc_ref[...], w[1, at, :], nt, preferred_element_type=f32
        ) + adapter_scale * lax.dot_general(mine, down[:, at], tn, preferred_element_type=f32)

    for c in low_copies:
        c.wait()

    @pl.loop(0, dp)
    def _(s):
        at = span(s, tokens)
        slots = low_all[s, 2 * rank :, :].astype(f32)
        spread_h[:, at] = spread(low_all[s, :rank, :].astype(f32), slots)
        spread_g[:, at] = spread(low_all[s, rank : 2 * rank, :].astype(f32), slots)

    for c in k_copies:
        c.wait()
    up_piece = adapter_scale * lax.dot_general(
        kct_all[...], spread_h[...], nt, preferred_element_type=f32
    )
    folds = pairs // cols
    for i in range(folds):
        gathered_ref[pairs + i * krows : pairs + (i + 1) * krows, span(me, cols)] = up_piece[
            :, i * cols : (i + 1) * cols
        ].astype(bf16)

    def finish_half(h):
        for c in x_copies[h]:
            c.wait()
        gathered_ref[:pairs, half_of(me, h)] = (
            adapter_scale
            * jnp.dot(
                spread_g[...], x_all[:, h * half : (h + 1) * half], preferred_element_type=f32
            )
        ).astype(bf16)

    pending, outs = [], []

    def block(src, h):
        return gathered_ref.at[:, half_of(src, h)]

    def index(zz, yy, cc):
        return (zz * 2 + yy) * 2 + cc

    def push(src, h, sems, i, to):
        c = remote(block(src, h), block(src, h), sems, i, (to, ten))
        c.start()
        pending.append(c)
        return c

    def put(src, h):
        c = pltpu.make_async_copy(
            gathered_ref.at[pl.ds(0, pairs), half_of(src, h)],
            down_out.at[:, half_of(src, h)],
            out_sem.at[len(outs)],
        )
        c.start()
        outs.append(c)

    right = index(lax.rem(z + 1, zn), y, core)
    left = index(lax.rem(z + zn - 1, zn), y, core)
    across = index(z, 1 - y, core)
    twin = index(z, y, 1 - core)
    z_copies, y_copies = {}, {}

    def layer(step, h):
        return lax.rem(z + (zn - step if h == 0 else step), zn)

    def ring(step, h):
        src = index(layer(step, h), y, core)
        if step > 0:
            z_copies[step - 1, h].wait_recv()
        i = 2 * step + h
        if step < zn - 1:
            z_copies[step, h] = push(src, h, z_sem, i, right if h == 0 else left)
        y_copies[step, h] = push(src, h, y_sem, i, across)
        push(src, h, c_sem, i, twin)
        put(src, h)

    def pass_on(step, h):
        y_copies[step, h].wait_recv()
        src = index(layer(step, h), 1 - y, core)
        push(src, h, c_sem, 2 * zn + 2 * step + h, twin)
        put(src, h)

    finish_half(0)
    ring(0, 0)
    ring(1, 0)
    pass_on(0, 0)
    finish_half(1)
    ring(0, 1)

    for c in f_copies:
        c.wait()

    @pl.loop(0, feats // chunk)
    def _(j):
        at = span(j, chunk)
        ingrad_ref[:, at] = (own_f[:, at] + recv_f[:, at].astype(f32)).astype(bf16)

    for step in range(2, zn + 1):
        if step < zn:
            ring(step, 0)
        pass_on(step - 1, 0)
        ring(step - 1, 1)
        pass_on(step - 2, 1)
    pass_on(zn - 1, 1)
    for yy in range(2):
        for step in range(zn):
            for h in range(2):
                i = 2 * zn * yy + 2 * step + h
                remote(block(0, 0), block(0, 0), c_sem, i, (twin, ten)).wait_recv()
                put(index(layer(step, h), y if yy == 0 else 1 - y, 1 - core), h)
    for i in range(folds):
        rows = gathered_ref[pairs + i * krows : pairs + (i + 1) * krows, :].astype(f32)
        stacked = jnp.concatenate([rows[:, p * cols : (p + 1) * cols] for p in range(dp)], axis=0)
        up_out[i * cols : (i + 1) * cols, :] = stacked.T.astype(bf16)
    for c in pending:
        c.wait_send()
    for c in outs:
        c.wait()


def per_device_kernel(
    dp,
    normed_input,
    key_cotangent,
    frozen_key_weight,
    adapter_down_maps,
    adapter_up_maps,
    document_of_token,
    tenant_of_document,
    tenant_slot_index,
):
    tenant_count, feats, rank = adapter_down_maps.shape
    heads = adapter_up_maps.shape[2]
    tokens = normed_input.shape[0]
    pairs = tenant_count * rank
    cols = feats // dp
    krows = heads // dp
    zn = dp // 4
    rows = pairs + krows * (pairs // cols)
    bf16, f32 = jnp.bfloat16, jnp.float32
    tenants = jnp.arange(tenant_count, dtype=jnp.int32)
    slot_of_doc = jnp.sum(
        jnp.where(tenant_of_document[:, None] == tenants[None, :], tenant_slot_index[None, :], 0), axis=1
    )
    docs = jnp.arange(tenant_of_document.shape[0], dtype=jnp.int32)
    slot = jnp.sum(
        jnp.where(document_of_token[None, :] == docs[:, None], slot_of_doc[:, None], 0),
        axis=0,
        keepdims=True,
    )
    down_rows = jnp.transpose(adapter_down_maps, (0, 2, 1)).reshape(pairs, feats)
    up_rows = adapter_up_maps.reshape(pairs, heads)
    vmem = pl.BlockSpec(memory_space=pltpu.VMEM)
    hbm = pl.BlockSpec(memory_space=pl.ANY)
    dma = pltpu.SemaphoreType.DMA
    down_flat, up_flat, input_gradient = pl.pallas_call(
        functools.partial(kernel, dp),
        out_shape=(
            jax.ShapeDtypeStruct((pairs, feats), bf16),
            jax.ShapeDtypeStruct((pairs, heads), bf16),
            jax.ShapeDtypeStruct((tokens, feats), bf16),
        ),
        in_specs=[vmem] * 5 + [hbm] * 2,
        out_specs=(hbm, vmem, vmem),
        scratch_shapes=[
            pltpu.VMEM((rows, feats), bf16),
            pltpu.VMEM((pairs, feats), bf16),
            pltpu.VMEM((2, feats, heads), bf16),
            pltpu.VMEM((tokens * dp, cols), bf16),
            pltpu.VMEM((krows, tokens * dp), bf16),
            pltpu.VMEM((2 * rank, tokens), f32),
            pltpu.VMEM((2 * rank, tokens), f32),
            pltpu.VMEM((dp, 3 * rank, tokens), bf16),
            pltpu.VMEM((pairs, tokens * dp), bf16),
            pltpu.VMEM((pairs, tokens * dp), bf16),
            pltpu.VMEM((tokens, feats), bf16),
            pltpu.VMEM((tokens, feats), bf16),
            pltpu.VMEM((tokens, feats), f32),
            dma((3,)),
            dma((2, 2 * dp)),
            dma((2, dp)),
            dma((2, 1)),
            dma((2, dp)),
            dma((2, 4)),
            dma((2, 2 * zn)),
            dma((2, 2 * zn)),
            dma((2, 4 * zn)),
            dma((2 * dp,)),
        ],
        compiler_params=pltpu.CompilerParams(
            collective_id=0, has_side_effects=True, vmem_limit_bytes=60 * 1024 * 1024
        ),
    )(
        normed_input,
        key_cotangent,
        key_cotangent.T,
        up_rows,
        slot,
        down_rows,
        frozen_key_weight,
    )
    down_gradient = jnp.transpose(
        down_flat.reshape(tenant_count, rank, feats), (0, 2, 1)
    )
    up_gradient = up_flat.reshape(tenant_count, rank, heads)
    return (input_gradient, down_gradient, up_gradient)


def fits_kernel(dp, tensor, args):
    tokens, feats = args[0].shape
    heads = args[1].shape[1]
    tenant_count, _, rank = args[3].shape
    pairs = tenant_count * rank
    if tensor != 2 or dp % 4 or dp < 8 or tokens != 128 or feats % (dp * 256) or heads % (dp * 16):
        return False
    cols = feats // dp
    rows = pairs + (heads // dp) * (pairs // cols)
    return (
        feats % 2048 == 0 and pairs % cols == 0 and rank % 16 == 0
        and rows % 32 == 0 and tenant_count <= 256
    )


def solution(mesh):
    in_specs = (
        P("dp", "tensor"),
        P("dp", "tensor"),
        P(None, "tensor"),
        P(None, "tensor", None),
        P(None, None, "tensor"),
        P("dp"),
        P(),
        P(),
    )
    out_specs = (P("dp", "tensor"), P(None, "tensor", None), P(None, None, "tensor"))

    def body(*args):
        dp, tensor = mesh.shape["dp"], mesh.shape["tensor"]
        if fits_kernel(dp, tensor, args):
            return per_device_kernel(dp, *args)
        return per_device(dp, tensor, *args)

    return jax.shard_map(body, mesh=mesh, in_specs=in_specs, out_specs=out_specs, check_vma=False)
```

```python
import functools
import jax
import jax.numpy as jnp
from jax import lax
from jax.experimental import pallas as pl
from jax.experimental.pallas import tpu as pltpu
from jax.sharding import PartitionSpec as P

adapter_scale = 2.0


def per_device(
    dp_count,
    tensor_count,
    normed_input,
    key_cotangent,
    frozen_key_weight,
    adapter_down_maps,
    adapter_up_maps,
    document_of_token,
    tenant_of_document,
    tenant_slot_index,
):
    tenant_count, token_rows, adapter_rank = adapter_down_maps.shape
    key_heads_width = adapter_up_maps.shape[2]
    tokens = normed_input.shape[0]
    doc_count = tenant_of_document.shape[0]
    pairs = tenant_count * adapter_rank
    bf16, f32 = jnp.bfloat16, jnp.float32
    tenants = jnp.arange(tenant_count, dtype=jnp.int32)
    slot_of_doc = jnp.sum(
        jnp.where(tenant_of_document[:, None] == tenants[None, :], tenant_slot_index[None, :], 0), axis=1
    )
    docs = jnp.arange(doc_count, dtype=jnp.int32)
    slot = jnp.sum(
        jnp.where(document_of_token[:, None] == docs[None, :], slot_of_doc[None, :], 0), axis=1
    )
    member = (slot[:, None] == tenants[None, :]).astype(f32)
    down_rows = jnp.transpose(adapter_down_maps, (0, 2, 1)).reshape(pairs, token_rows)
    up_rows = adapter_up_maps.reshape(pairs, key_heads_width)
    contract_last = (((1,), (1,)), ((), ()))
    h_all = lax.dot_general(normed_input, down_rows, contract_last, preferred_element_type=f32)
    g_all = lax.dot_general(key_cotangent, up_rows, contract_last, preferred_element_type=f32)
    h_part = jnp.sum(h_all.reshape(-1, tenant_count, adapter_rank) * member[:, :, None], axis=1)
    g_part = jnp.sum(g_all.reshape(-1, tenant_count, adapter_rank) * member[:, :, None], axis=1)
    low = lax.psum(jnp.concatenate([h_part, g_part], axis=1), "tensor").astype(bf16)

    x_all = lax.all_to_all(
        normed_input.reshape(tokens, dp_count, -1), "dp", split_axis=1, concat_axis=0, tiled=True
    ).reshape(tokens * dp_count, -1)
    k_all = lax.all_to_all(
        key_cotangent.reshape(tokens, dp_count, -1), "dp", split_axis=1, concat_axis=0, tiled=True
    ).reshape(tokens * dp_count, -1)
    tagged = jnp.concatenate([low, slot[:, None].astype(bf16)], axis=1)
    tagged_all = lax.all_gather(tagged, "dp", axis=0, tiled=True)
    slot_all = tagged_all[:, 2 * adapter_rank].astype(jnp.int32)
    member_all = (slot_all[:, None] == tenants[None, :]).astype(bf16)

    def spread(m, v):
        return (m[:, :, None] * v[:, None, :]).reshape(-1, pairs)

    spread_h = spread(member_all, tagged_all[:, :adapter_rank])
    spread_g_all = spread(member_all, tagged_all[:, adapter_rank : 2 * adapter_rank])
    contract_first = (((0,), (0,)), ((), ()))
    down_piece = (
        adapter_scale * lax.dot_general(spread_g_all, x_all, contract_first, preferred_element_type=f32)
    ).astype(bf16)
    up_piece = (
        adapter_scale * lax.dot_general(spread_h, k_all, contract_first, preferred_element_type=f32)
    ).astype(bf16)
    down_flat = lax.all_gather(down_piece, "dp", axis=1, tiled=True)
    up_flat = lax.all_gather(up_piece, "dp", axis=1, tiled=True)

    frozen = lax.dot_general(
        key_cotangent, frozen_key_weight, contract_last, preferred_element_type=f32
    )
    frozen_output = lax.psum_scatter(frozen.astype(bf16), "tensor", scatter_dimension=1, tiled=True)
    spread_g = spread(member.astype(bf16), low[:, adapter_rank:])
    adapter_output = jnp.dot(spread_g, down_rows, preferred_element_type=f32)
    input_gradient = (frozen_output.astype(f32) + adapter_scale * adapter_output).astype(bf16)
    down_gradient = jnp.transpose(
        down_flat.reshape(tenant_count, adapter_rank, token_rows), (0, 2, 1)
    )
    up_gradient = up_flat.reshape(tenant_count, adapter_rank, key_heads_width)
    return (input_gradient, down_gradient, up_gradient)


MESH = pl.DeviceIdType.MESH


def kernel(
    dp,
    x_ref, kc_ref, up_ref, doc_ref, tenant_ref, index_ref, down_hbm, w_hbm,
    down_out, up_out, ingrad_ref,
    kct_ref, gathered_ref, down, w, x_all, kct_all, part, part_in, low_all, spread_h, spread_g, send_f, recv_f, own_f,
    local_sem, x_sem, k_sem, part_sem, low_sem, f_sem, z_sem, y_sem, c_sem, out_sem,
):
    bf16, f32 = jnp.bfloat16, jnp.float32
    tokens, feats = x_ref.shape
    pairs = down.shape[0]
    heads = kc_ref.shape[1]
    rank = part.shape[0] // 2
    tenants = pairs // rank
    cols = feats // dp
    krows = heads // dp
    me = lax.axis_index("dp")
    ten = lax.axis_index("tensor")
    other = 1 - ten
    zn = dp // 4
    z, y, core = me // 4, (me // 2) % 2, me % 2

    def w_half(t, i):
        rows = pl.ds(pl.multiple_of(t * feats, feats), feats)
        return pltpu.make_async_copy(w_hbm.at[rows], w.at[i], local_sem.at[i])

    load_down = pltpu.make_async_copy(down_hbm, down, local_sem.at[2])
    load_down.start()
    load_other = w_half(other, 0)
    load_other.start()
    load_own = w_half(ten, 1)
    load_own.start()

    kct_ref[...] = kc_ref[...].astype(f32).T.astype(bf16)
    barrier = pltpu.get_barrier_semaphore()
    for o in range(1, dp):
        pl.semaphore_signal(
            barrier, inc=1, device_id=(lax.rem(me + o, dp), ten), device_id_type=MESH
        )
    pl.semaphore_signal(barrier, inc=1, device_id=(me, other), device_id_type=MESH)
    pl.semaphore_wait(barrier, dp)

    def remote(src, dst, sems, i, to):
        return pltpu.make_async_remote_copy(
            src_ref=src, dst_ref=dst, send_sem=sems.at[0, i], recv_sem=sems.at[1, i],
            device_id=to, device_id_type=MESH,
        )

    def span(i, n):
        return pl.ds(pl.multiple_of(i * n, n), n)

    half = cols // 2

    def half_of(src, h):
        return pl.ds(pl.multiple_of(src * cols + h * half, half), half)

    x_copies, k_copies = [[], []], []
    for o in range(1, dp):
        p = lax.rem(me + o, dp)
        c = remote(
            kct_ref.at[span(p, krows)], kct_all.at[:, span(me, tokens)], k_sem, o, (p, ten)
        )
        c.start()
        k_copies.append(c)
    for h in range(2):
        for o in range(1, dp):
            p = lax.rem(me + o, dp)
            c = remote(
                x_ref.at[:, half_of(p, h)],
                x_all.at[h, span(me, tokens)],
                x_sem,
                h * dp + o,
                (p, ten),
            )
            c.start()
            x_copies[h].append(c)
    for h in range(2):
        x_all[h, span(me, tokens), :] = x_ref[:, half_of(me, h)]
    kct_all[:, span(me, tokens)] = kct_ref[span(me, krows), :]

    nt = (((1,), (1,)), ((), ()))
    slots_now = jnp.zeros((1, tokens), jnp.int32)
    for d in range(tenant_ref.shape[0]):
        slots_now = jnp.where(doc_ref[...] == d, index_ref[tenant_ref[d]], slots_now)
    slot_row = slots_now.astype(f32)
    tenant_of_row = lax.broadcasted_iota(jnp.int32, (tenants, rank, tokens), 0).astype(f32)

    def pick(values):
        v = values.reshape(tenants, rank, tokens)
        return jnp.sum(jnp.where(tenant_of_row == slot_row[None], v, 0.0), axis=0)

    def spread(values, slots):
        full = jnp.where(tenant_of_row == slots[None], values[None], 0.0)
        return full.astype(bf16).reshape(pairs, tokens)

    part[rank:, :] = pick(lax.dot_general(up_ref[...], kc_ref[...], nt, preferred_element_type=f32))
    load_down.wait()
    part[:rank, :] = pick(lax.dot_general(down[...], x_ref[...], nt, preferred_element_type=f32))
    part_copy = remote(part, part_in, part_sem, 0, (me, other))
    part_copy.start()

    chunk = 512
    groups = f_sem.shape[1]
    per_group = feats // chunk // groups
    load_other.wait()
    f_copies = []
    for g in range(groups):

        @pl.loop(g * per_group, (g + 1) * per_group)
        def _(j):
            at = span(j, chunk)
            send_f[:, at] = lax.dot_general(
                kc_ref[...], w[0, at, :], nt, preferred_element_type=f32
            ).astype(bf16)

        width = per_group * chunk
        at = pl.ds(g * width, width)
        c = remote(send_f.at[:, at], recv_f.at[:, at], f_sem, g, (me, other))
        c.start()
        f_copies.append(c)

    part_copy.wait()
    total = part[...] + part_in[...]
    low_all[me, : 2 * rank, :] = total.astype(bf16)
    low_all[me, 2 * rank :, :] = jnp.broadcast_to(slot_row, (rank, tokens)).astype(bf16)
    low_copies = []
    for o in range(1, dp):
        c = remote(low_all.at[me], low_all.at[me], low_sem, o, (lax.rem(me + o, dp), ten))
        c.start()
        low_copies.append(c)

    low_g = total[rank:, :].astype(bf16).astype(f32)
    mine = spread(low_g, jnp.broadcast_to(slot_row, (rank, tokens)))
    tn = (((0,), (0,)), ((), ()))
    load_own.wait()

    @pl.loop(0, feats // chunk)
    def _(j):
        at = span(j, chunk)
        own_f[:, at] = lax.dot_general(
            kc_ref[...], w[1, at, :], nt, preferred_element_type=f32
        ) + adapter_scale * lax.dot_general(mine, down[:, at], tn, preferred_element_type=f32)

    for c in low_copies:
        c.wait()

    @pl.loop(0, dp)
    def _(s):
        at = span(s, tokens)
        slots = low_all[s, 2 * rank :, :].astype(f32)
        spread_h[:, at] = spread(low_all[s, :rank, :].astype(f32), slots)
        spread_g[:, at] = spread(low_all[s, rank : 2 * rank, :].astype(f32), slots)

    for c in k_copies:
        c.wait()
    up_piece = adapter_scale * lax.dot_general(
        kct_all[...], spread_h[...], nt, preferred_element_type=f32
    )
    folds = pairs // cols
    for i in range(folds):
        for h in range(2):
            gathered_ref[me, h, pairs + i * krows : pairs + (i + 1) * krows, :] = up_piece[
                :, i * cols + h * half : i * cols + (h + 1) * half
            ].astype(bf16)

    def finish_half(h):
        for c in x_copies[h]:
            c.wait()
        gathered_ref[me, h, :pairs, :] = (
            adapter_scale
            * jnp.dot(
                spread_g[...], x_all[h], preferred_element_type=f32
            )
        ).astype(bf16)

    pending, outs = [], []

    def block(src, h):
        return gathered_ref.at[src, h]

    def index(zz, yy, cc):
        return (zz * 2 + yy) * 2 + cc

    def push(src, h, sems, i, to):
        c = remote(block(src, h), block(src, h), sems, i, (to, ten))
        c.start()
        pending.append(c)
        return c

    def put(src, h):
        c = pltpu.make_async_copy(
            gathered_ref.at[src, h, pl.ds(0, pairs)],
            down_out.at[:, half_of(src, h)],
            out_sem.at[len(outs)],
        )
        c.start()
        outs.append(c)

    right = index(lax.rem(z + 1, zn), y, core)
    left = index(lax.rem(z + zn - 1, zn), y, core)
    across = index(z, 1 - y, core)
    twin = index(z, y, 1 - core)
    z_copies, y_copies = {}, {}

    def layer(step, h):
        return lax.rem(z + (zn - step if h == 0 else step), zn)

    def ring(step, h):
        src = index(layer(step, h), y, core)
        if step > 0:
            z_copies[step - 1, h].wait_recv()
        i = 2 * step + h
        if step < zn - 1:
            z_copies[step, h] = push(src, h, z_sem, i, right if h == 0 else left)
        y_copies[step, h] = push(src, h, y_sem, i, across)
        push(src, h, c_sem, i, twin)
        put(src, h)

    def pass_on(step, h):
        y_copies[step, h].wait_recv()
        src = index(layer(step, h), 1 - y, core)
        push(src, h, c_sem, 2 * zn + 2 * step + h, twin)
        put(src, h)

    finish_half(0)
    ring(0, 0)
    ring(1, 0)
    pass_on(0, 0)
    finish_half(1)
    ring(0, 1)

    for c in f_copies:
        c.wait()

    @pl.loop(0, feats // chunk)
    def _(j):
        at = span(j, chunk)
        ingrad_ref[:, at] = (own_f[:, at] + recv_f[:, at].astype(f32)).astype(bf16)

    for step in range(2, zn + 1):
        if step < zn:
            ring(step, 0)
        pass_on(step - 1, 0)
        ring(step - 1, 1)
        pass_on(step - 2, 1)
    pass_on(zn - 1, 1)
    for yy in range(2):
        for step in range(zn):
            for h in range(2):
                i = 2 * zn * yy + 2 * step + h
                remote(block(0, 0), block(0, 0), c_sem, i, (twin, ten)).wait_recv()
                put(index(layer(step, h), y if yy == 0 else 1 - y, 1 - core), h)
    for i in range(folds):
        at = slice(pairs + i * krows, pairs + (i + 1) * krows)
        stacked = jnp.concatenate(
            [
                jnp.concatenate(
                    [gathered_ref[p, h, at, :].astype(f32) for p in range(dp)], axis=0
                )
                for h in range(2)
            ],
            axis=1,
        )
        up_out[i * cols : (i + 1) * cols, :] = stacked.T.astype(bf16)
    for c in pending:
        c.wait_send()
    for c in outs:
        c.wait()


def per_device_kernel(
    dp,
    normed_input,
    key_cotangent,
    frozen_key_weight,
    adapter_down_maps,
    adapter_up_maps,
    document_of_token,
    tenant_of_document,
    tenant_slot_index,
):
    tenant_count, feats, rank = adapter_down_maps.shape
    heads = adapter_up_maps.shape[2]
    tokens = normed_input.shape[0]
    pairs = tenant_count * rank
    cols = feats // dp
    krows = heads // dp
    zn = dp // 4
    rows = pairs + krows * (pairs // cols)
    bf16, f32 = jnp.bfloat16, jnp.float32
    down_rows = jnp.transpose(adapter_down_maps, (0, 2, 1)).reshape(pairs, feats)
    up_rows = adapter_up_maps.reshape(pairs, heads)
    vmem = pl.BlockSpec(memory_space=pltpu.VMEM)
    smem = pl.BlockSpec(memory_space=pltpu.SMEM)
    hbm = pl.BlockSpec(memory_space=pltpu.HBM)
    anywhere = pl.BlockSpec(memory_space=pl.ANY)
    dma = pltpu.SemaphoreType.DMA
    down_flat, up_flat, input_gradient = pl.pallas_call(
        functools.partial(kernel, dp),
        out_shape=(
            jax.ShapeDtypeStruct((pairs, feats), bf16),
            jax.ShapeDtypeStruct((pairs, heads), bf16),
            jax.ShapeDtypeStruct((tokens, feats), bf16),
        ),
        in_specs=[vmem] * 4 + [smem] * 2 + [hbm] * 2,
        out_specs=(anywhere, vmem, vmem),
        scratch_shapes=[
            pltpu.VMEM((heads, tokens), bf16),
            pltpu.VMEM((dp, 2, rows, cols // 2), bf16),
            pltpu.VMEM((pairs, feats), bf16),
            pltpu.VMEM((2, feats, heads), bf16),
            pltpu.VMEM((2, tokens * dp, cols // 2), bf16),
            pltpu.VMEM((krows, tokens * dp), bf16),
            pltpu.VMEM((2 * rank, tokens), f32),
            pltpu.VMEM((2 * rank, tokens), f32),
            pltpu.VMEM((dp, 3 * rank, tokens), bf16),
            pltpu.VMEM((pairs, tokens * dp), bf16),
            pltpu.VMEM((pairs, tokens * dp), bf16),
            pltpu.VMEM((tokens, feats), bf16),
            pltpu.VMEM((tokens, feats), bf16),
            pltpu.VMEM((tokens, feats), f32),
            dma((3,)),
            dma((2, 2 * dp)),
            dma((2, dp)),
            dma((2, 1)),
            dma((2, dp)),
            dma((2, 4)),
            dma((2, 2 * zn)),
            dma((2, 2 * zn)),
            dma((2, 4 * zn)),
            dma((2 * dp,)),
        ],
        compiler_params=pltpu.CompilerParams(
            collective_id=0, has_side_effects=True, vmem_limit_bytes=40 * 1024 * 1024
        ),
    )(
        normed_input,
        key_cotangent,
        up_rows,
        document_of_token.reshape(1, tokens),
        tenant_of_document,
        tenant_slot_index,
        down_rows,
        frozen_key_weight,
    )
    down_gradient = jnp.transpose(
        down_flat.reshape(tenant_count, rank, feats), (0, 2, 1)
    )
    up_gradient = up_flat.reshape(tenant_count, rank, heads)
    return (input_gradient, down_gradient, up_gradient)


def fits_kernel(dp, tensor, args):
    tokens, feats = args[0].shape
    heads = args[1].shape[1]
    tenant_count, _, rank = args[3].shape
    pairs = tenant_count * rank
    if tensor != 2 or dp % 4 or dp < 8 or tokens != 128 or feats % (dp * 256) or heads % (dp * 16):
        return False
    cols = feats // dp
    rows = pairs + (heads // dp) * (pairs // cols)
    return (
        feats % 2048 == 0 and pairs % cols == 0 and rank % 16 == 0
        and rows % 32 == 0 and tenant_count <= 256
    )


def solution(mesh):
    in_specs = (
        P("dp", "tensor"),
        P("dp", "tensor"),
        P(None, "tensor"),
        P(None, "tensor", None),
        P(None, None, "tensor"),
        P("dp"),
        P(),
        P(),
    )
    out_specs = (P("dp", "tensor"), P(None, "tensor", None), P(None, None, "tensor"))

    def body(*args):
        dp, tensor = mesh.shape["dp"], mesh.shape["tensor"]
        if fits_kernel(dp, tensor, args):
            return per_device_kernel(dp, *args)
        return per_device(dp, tensor, *args)

    return jax.shard_map(body, mesh=mesh, in_specs=in_specs, out_specs=out_specs, check_vma=False)
```
